32 devices in a mesh: seq: 8 (over y, x, core), head: 4 (over z).
Axes of the slice: x: 2, y: 2, z: 4, core: 2. Of those that a mesh axis runs over, the one named last changes fastest.
Arguments:
- queries: bfloat16 [8192, 2048], P(('seq', 'head')), may hold values from -15 to 15
- key_rows: bfloat16 [8192, 2048], P(('seq', 'head')), may hold values from -15 to 15
- values: bfloat16 [8192, 2048], P(('seq', 'head')), may hold values from -6 to 6
- gate_logits: float32 [16], P('head'), may hold values from -1.5 to 1.5
- out_grad: bfloat16 [8192, 2048], P(('seq', 'head')), may hold values from -6 to 6
Outputs:
- output: bfloat16 [8192, 2048], P(('seq', 'head'))
- query_grad: bfloat16 [8192, 2048], P(('seq', 'head'))
- key_grad: bfloat16 [8192, 2048], P(('seq', 'head'))
- value_grad: bfloat16 [8192, 2048], P(('seq', 'head'))
The draws below stay inside these ranges and needn't reach their ends.
All inputs are finite; a program needn't handle non-finite values.
Results may differ from the reference program's by a relative error of at most 0.0052.
The reference program's roundings to bfloat16 on the way count: a program that leaves them out, or rounds other values in their place, can miss the bound.
Values may be sent and summed in bfloat16 or wider, within the bound.
A program may use at most 128 MiB of HBM per device.

```python
import jax
import jax.numpy as jnp
from jax import lax

HEADS = 16
DH = 128
SEG = 1024
SEGMENTS = 8
TOKENS = 8192


def drawn_pair(key):
    base = jax.random.fold_in(key, 101)
    key_query, key_keys = jax.random.split(base, 2)
    full_shape = (TOKENS, HEADS * DH)
    query_draw = jnp.clip(jax.random.normal(key_query, full_shape, jnp.float32), -3.0, 3.0)
    key_draw = jnp.clip(jax.random.normal(key_keys, full_shape, jnp.float32), -3.0, 3.0)
    return (query_draw, key_draw)


def shifted(key, salt):
    key_noise, key_offset = jax.random.split(jax.random.fold_in(key, salt))
    full_shape = (SEGMENTS, SEG, HEADS * DH)
    noise = jnp.clip(jax.random.normal(key_noise, full_shape, jnp.float32), -3.0, 3.0)
    offset = jnp.clip(jax.random.normal(key_offset, (SEGMENTS, 1, HEADS * DH), jnp.float32), -3.0, 3.0)
    return (noise + offset).reshape(TOKENS, HEADS * DH)


def draw_queries(key, part):
    return drawn_pair(key)[0].astype(jnp.bfloat16)


def draw_key_rows(key, part):
    return drawn_pair(key)[1].astype(jnp.bfloat16)


def draw_values(key, part):
    return shifted(key, 202).astype(jnp.bfloat16)


def draw_out_grad(key, part):
    return shifted(key, 303).astype(jnp.bfloat16)


def shard_levels(rng, extent, cuts, least, top_value):
    def one(axis_at, blocks):
        heights = jax.random.uniform(jax.random.fold_in(jax.random.fold_in(rng, 6), axis_at), (blocks,), jnp.float32, least / len(cuts), top_value / len(cuts))
        return jnp.repeat(jnp.exp(heights), extent[axis_at] // blocks).reshape((-1,) + (1,) * (len(extent) - axis_at - 1))

    factor_of = one(*cuts[0])
    for cut in cuts[1:]:
        factor_of = factor_of * one(*cut)
    return factor_of


def setup_inputs(seed: int = 0) -> dict:
    splits = jax.random.split(jax.random.key(seed), 6)
    return {
        "queries": draw_queries(jax.random.fold_in(splits[5], 71), 0),
        "key_rows": draw_key_rows(jax.random.fold_in(splits[5], 71), 0),
        "values": draw_values(jax.random.fold_in(splits[5], 71), 0),
        "gate_logits": jnp.clip(jax.random.uniform(splits[3], (HEADS,), jnp.float32, -1.5, 1.5) * shard_levels(splits[3], (HEADS,), ((0, 4),), -0.4, 0.0), -1.5, 1.5),
        "out_grad": draw_out_grad(jax.random.fold_in(splits[5], 71), 0),
    }


highest = lax.Precision.HIGHEST


def feature(inputs):
    return jnp.where(inputs > 0, inputs + 1.0, jnp.exp(jnp.minimum(inputs, 0.0)))


def feature_slope(inputs):
    return jnp.where(inputs > 0, jnp.ones_like(inputs), jnp.exp(jnp.minimum(inputs, 0.0)))


def rounded(inputs):
    return lax.optimization_barrier(inputs.astype(jnp.bfloat16)).astype(jnp.float32)


def memory_part(query_seg, grad_seg, memory, normalizer, gate_share):
    phi_queries = rounded(feature(query_seg.astype(jnp.float32)))
    numerator = jnp.einsum("thd,hde->the", phi_queries, memory, precision=highest)
    raw_denom = jnp.einsum("thd,hd->th", phi_queries, normalizer, precision=highest)
    denominator = jnp.maximum(raw_denom, 1.0)
    retrieved = numerator / denominator[:, :, None]
    grad_wide = grad_seg.astype(jnp.float32)
    numer_grad = gate_share[None, :, None] * grad_wide / denominator[:, :, None]
    denom_grad = jnp.where(raw_denom > 1.0, -gate_share[None, :] * jnp.sum(grad_wide * retrieved, axis=-1) / denominator, 0.0)
    memory_grad = jnp.einsum("thd,the->hde", phi_queries, numer_grad, precision=highest)
    norm_grad = jnp.einsum("th,thd->hd", denom_grad, phi_queries, precision=highest)
    return retrieved, numer_grad, denom_grad, memory_grad, norm_grad


def local_head(inputs):
    query_part, key_part, value_part, grad_part, share = inputs
    score_scale = DH ** -0.5
    scores = jnp.dot(query_part, key_part.T, preferred_element_type=jnp.float32) * score_scale
    causal = jnp.arange(SEG)[:, None] >= jnp.arange(SEG)[None, :]
    scores = jnp.where(causal, scores, -jnp.inf)
    row_max = jnp.max(scores, axis=-1, keepdims=True)
    exp_scores = jnp.exp(scores - row_max)
    weights = exp_scores / jnp.sum(exp_scores, axis=-1, keepdims=True)
    weights_low = weights.astype(jnp.bfloat16)
    local = jnp.dot(weights_low, value_part, preferred_element_type=jnp.float32)
    weight_grad = jnp.dot(grad_part, value_part.T, preferred_element_type=jnp.float32) * (1.0 - share)
    score_grad = weights * (weight_grad - jnp.sum(weights * weight_grad, axis=-1, keepdims=True))
    score_low = score_grad.astype(jnp.bfloat16)
    query_local = jnp.dot(score_low, key_part, preferred_element_type=jnp.float32) * score_scale
    key_local = jnp.dot(score_low.T, query_part, preferred_element_type=jnp.float32) * score_scale
    value_local = jnp.dot(weights_low.T, grad_part, preferred_element_type=jnp.float32) * (1.0 - share)
    return local, query_local, key_local, value_local


def reference(queries, key_rows, values, gate_logits, out_grad):
    full_shape = (SEGMENTS, SEG, HEADS, DH)
    query_all = queries.reshape(full_shape)
    key_all = key_rows.reshape(full_shape)
    value_all = values.reshape(full_shape)
    grad_all = out_grad.reshape(full_shape)
    gate_share = jax.nn.sigmoid(gate_logits.astype(jnp.float32))

    def segment_update(inputs):
        key_seg, value_seg = inputs
        phi_keys = rounded(feature(key_seg.astype(jnp.float32)))
        update = jnp.einsum("thd,the->hde", phi_keys, value_seg.astype(jnp.float32), precision=highest)
        return update, jnp.sum(phi_keys, axis=0)

    updates, key_sums = lax.map(segment_update, (key_all, value_all))
    memory_all = jnp.concatenate([jnp.zeros_like(updates[:1]), jnp.cumsum(updates, axis=0)[:-1]], axis=0)
    normal_all = jnp.concatenate([jnp.zeros_like(key_sums[:1]), jnp.cumsum(key_sums, axis=0)[:-1]], axis=0)

    def segment_grads(inputs):
        query_seg, grad_seg, memory, normalizer = inputs
        parts = memory_part(query_seg, grad_seg, memory, normalizer, gate_share)
        return parts[3], parts[4]

    memory_grads, norm_grads = lax.map(segment_grads, (query_all, grad_all, memory_all, normal_all))
    later_memory = jnp.cumsum(memory_grads[::-1], axis=0)[::-1]
    later_norm = jnp.cumsum(norm_grads[::-1], axis=0)[::-1]
    back_memory_all = jnp.concatenate([later_memory[1:], jnp.zeros_like(later_memory[:1])], axis=0)
    back_norm_all = jnp.concatenate([later_norm[1:], jnp.zeros_like(later_norm[:1])], axis=0)

    def segment_pass(inputs):
        query_seg, key_seg, value_seg, grad_seg, memory, normalizer, back_memory, back_norm = inputs
        retrieved, numer_grad, denom_grad, unused_memory, unused_norm = memory_part(query_seg, grad_seg, memory, normalizer, gate_share)
        local, query_local, key_local, value_local = lax.map(local_head, (query_seg.transpose(1, 0, 2), key_seg.transpose(1, 0, 2), value_seg.transpose(1, 0, 2), grad_seg.transpose(1, 0, 2), gate_share))
        local = local.transpose(1, 0, 2)
        share = gate_share[None, :, None]
        output = (share * retrieved + (1.0 - share) * local).astype(jnp.bfloat16)
        query_wide = query_seg.astype(jnp.float32)
        key_wide = key_seg.astype(jnp.float32)
        value_wide = value_seg.astype(jnp.float32)
        query_grad = query_local.transpose(1, 0, 2) + (jnp.einsum("the,hde->thd", numer_grad, memory, precision=highest) + denom_grad[:, :, None] * normalizer[None]) * feature_slope(query_wide)
        key_grad = key_local.transpose(1, 0, 2) + (jnp.einsum("the,hde->thd", value_wide, back_memory, precision=highest) + back_norm[None]) * feature_slope(key_wide)
        phi_keys = rounded(feature(key_wide))
        value_grad = value_local.transpose(1, 0, 2) + jnp.einsum("thd,hde->the", phi_keys, back_memory, precision=highest)
        return output, query_grad.astype(jnp.bfloat16), key_grad.astype(jnp.bfloat16), value_grad.astype(jnp.bfloat16)

    results = lax.map(segment_pass, (query_all, key_all, value_all, grad_all, memory_all, normal_all, back_memory_all, back_norm_all))
    output, query_grad, key_grad, value_grad = [part.reshape(TOKENS, HEADS * DH) for part in results]
    return (output, query_grad, key_grad, value_grad)
```

```python
import functools

import jax
import jax.numpy as jnp
from jax import lax
from jax.experimental import pallas as pl
from jax.experimental.pallas import tpu as pltpu
from jax.sharding import PartitionSpec as P

DH = 128
PAD = 8
MESH = pl.DeviceIdType.MESH
F32 = jnp.float32
BF16 = jnp.bfloat16


def feature(x):
    return jnp.where(x > 0, x + 1.0, jnp.exp(jnp.minimum(x, 0.0)))


def slope(x):
    return jnp.where(x > 0, 1.0, jnp.exp(jnp.minimum(x, 0.0)))


def split(x):
    high = x.astype(BF16)
    return high, (x - high.astype(F32)).astype(BF16)


def nn(a, b):
    return lax.dot_general(a, b, (((1,), (0,)), ((), ())), preferred_element_type=F32)


def nt(a, b):
    return lax.dot_general(a, b, (((1,), (1,)), ((), ())), preferred_element_type=F32)


def tn(a, b):
    return lax.dot_general(a, b, (((0,), (0,)), ((), ())), preferred_element_type=F32)


def kernel(
    segs,
    groups,
    heads,
    gate_ref,
    q_in,
    k_in,
    v_in,
    d_in,
    o_out,
    q_out,
    k_out,
    v_out,
    gath,
    stage,
    loc,
    fwd_mine,
    fwd_slots,
    bwd_mine,
    bwd_slots,
    carry,
    in_send,
    in_recv,
    out_send,
    out_recv,
    fwd_send,
    fwd_recv,
    bwd_send,
    bwd_recv,
):
    seg = lax.axis_index("seq")
    grp = lax.axis_index("head")
    rows = q_in.shape[0]
    length = rows * groups
    inputs = (k_in, v_in, q_in, d_in)
    outputs = (o_out, q_out, k_out, v_out)
    scale = DH ** (-0.5)
    offsets = sorted(range(1, groups), key=lambda o: abs(2 * o - groups))

    barrier = pltpu.get_barrier_semaphore()
    for o in range(1, groups):
        pl.semaphore_signal(
            barrier, inc=1, device_id=(seg, lax.rem(grp + o, groups)), device_id_type=MESH
        )

    def greet(o, c):
        pl.semaphore_signal(
            barrier, inc=1, device_id=(lax.rem(seg + o, segs), grp), device_id_type=MESH
        )
        return c

    lax.fori_loop(1, segs, greet, 0)
    pl.semaphore_wait(barrier, groups - 1 + segs - 1)

    def in_copy(a, h, dest):
        col = pl.multiple_of((dest * heads + h) * DH, DH)
        at = pl.multiple_of(grp * rows, rows)
        return (
            inputs[a].at[:, pl.ds(col, DH)],
            gath.at[a, h, pl.ds(at, rows), :],
        )

    def send_inputs(h, c):
        for a in range(4):
            for o in offsets:
                dest = lax.rem(grp + o, groups)
                src, dst = in_copy(a, h, dest)
                pltpu.make_async_remote_copy(
                    src_ref=src,
                    dst_ref=dst,
                    send_sem=in_send.at[a, h, dest],
                    recv_sem=in_recv.at[a, h, grp],
                    device_id=(seg, dest),
                    device_id_type=MESH,
                ).start()
            src, dst = in_copy(a, h, grp)
            pltpu.make_async_copy(src, dst, in_recv.at[a, h, grp]).start()
        return c

    lax.fori_loop(0, heads, send_inputs, 0)

    def wait_inputs(a, h):
        def one(z, c):
            blk = gath.at[a, h, pl.ds(pl.multiple_of(z * rows, rows), rows), :]
            pltpu.make_async_copy(blk, blk, in_recv.at[a, h, z]).wait()
            return c

        lax.fori_loop(0, groups, one, 0)

    def send_out(a, h):
        col = pl.multiple_of((grp * heads + h) * DH, DH)
        for o in offsets:
            dest = lax.rem(grp + o, groups)
            pltpu.make_async_remote_copy(
                src_ref=stage.at[a, h, pl.ds(pl.multiple_of(dest * rows, rows), rows), :],
                dst_ref=outputs[a].at[:, pl.ds(col, DH)],
                send_sem=out_send.at[a, h, dest],
                recv_sem=out_recv.at[a, h, grp],
                device_id=(seg, dest),
                device_id_type=MESH,
            ).start()
        pltpu.make_async_copy(
            stage.at[a, h, pl.ds(pl.multiple_of(grp * rows, rows), rows), :],
            outputs[a].at[:, pl.ds(col, DH)],
            out_recv.at[a, h, grp],
        ).start()

    def gate(h):
        return gate_ref[h][:1, :]

    def part_update(h):
        wait_inputs(0, h)
        wait_inputs(1, h)
        phi = feature(gath[0, h].astype(F32)).astype(BF16)
        fwd_mine[h, :DH, :] = tn(phi, gath[1, h])
        fwd_mine[h, DH:, :] = jnp.broadcast_to(
            jnp.sum(phi.astype(F32), axis=0, keepdims=True), (PAD, DH)
        )

        def one(j, c):
            pltpu.make_async_remote_copy(
                src_ref=fwd_mine.at[h],
                dst_ref=fwd_slots.at[h, seg],
                send_sem=fwd_send.at[h, j],
                recv_sem=fwd_recv.at[h, seg],
                device_id=(j, grp),
                device_id_type=MESH,
            ).start()
            return c

        lax.fori_loop(seg + 1, segs, one, 0)

    def part_local(h):
        wait_inputs(2, h)
        wait_inputs(3, h)
        rest = 1.0 - gate(h)[:, :1]
        for i in range(groups - 1, -1, -1):
            first, wide = i * rows, (i + 1) * rows
            q = gath[2, h, first:wide, :]
            d = gath[3, h, first:wide, :]
            k = gath[0, h, :wide, :]
            v = gath[1, h, :wide, :]
            s = nt(q, k) * scale
            row = lax.broadcasted_iota(jnp.int32, (rows, wide), 0) + first
            col = lax.broadcasted_iota(jnp.int32, (rows, wide), 1)
            s = jnp.where(row >= col, s, -jnp.inf)
            e = jnp.exp(s - jnp.max(s, axis=-1, keepdims=True))
            w = e * (1.0 / jnp.sum(e, axis=-1, keepdims=True))
            wb = w.astype(BF16)
            dp = nt(d, v) * rest
            ds = w * (dp - jnp.sum(w * dp, axis=-1, keepdims=True))
            dsb = ds.astype(BF16)
            loc[0, h, first:wide, :] = nn(wb, v)
            loc[1, h, first:wide, :] = nn(dsb, k)
            kg = tn(dsb, q)
            vg = tn(wb, d)
            if i == groups - 1:
                loc[2, h] = kg
                loc[3, h] = vg
            else:
                loc[2, h, :wide, :] += kg
                loc[3, h, :wide, :] += vg

    def part_memory(h):
        carry[...] = jnp.zeros_like(carry)

        def one(j, c):
            slot = fwd_slots.at[h, j]
            pltpu.make_async_copy(slot, slot, fwd_recv.at[h, j]).wait()
            carry[...] += fwd_slots[h, j]
            return c

        lax.fori_loop(0, seg, one, 0)
        memory, zsum = carry[:DH, :], carry[DH : DH + 1, :]
        high, low = split(memory)
        g = gate(h)
        update = jnp.zeros((DH, DH), F32)
        norm = jnp.zeros((1, DH), F32)
        for i in range(groups):
            here = slice(i * rows, (i + 1) * rows)
            q = gath[2, h, here, :].astype(F32)
            d = gath[3, h, here, :]
            wide = d.astype(F32)
            phi = feature(q).astype(BF16)
            phi_wide = phi.astype(F32)
            raw = jnp.sum(phi_wide * zsum, axis=-1, keepdims=True)
            inv = 1.0 / jnp.maximum(raw, 1.0)
            retrieved = (nn(phi, high) + nn(phi, low)) * inv
            factor = g * inv
            numer = factor * wide
            denom = jnp.where(
                raw > 1.0,
                -g * jnp.sum(wide * retrieved, axis=-1, keepdims=True) * inv,
                0.0,
            )
            numer_high, numer_low = split(numer)
            update = update + tn(phi, numer_high) + tn(phi, numer_low)
            norm = norm + jnp.sum(denom * phi_wide, axis=0, keepdims=True)
            stage[0, h, here, :] = (g * retrieved + (1.0 - g) * loc[0, h, here, :]).astype(BF16)
            back = (nt(d, high) + nt(d, low)) * factor + denom * zsum
            stage[1, h, here, :] = (loc[1, h, here, :] * scale + back * slope(q)).astype(BF16)
        bwd_mine[h, :DH, :] = update
        bwd_mine[h, DH:, :] = jnp.broadcast_to(norm, (PAD, DH))

        def give(j, c):
            pltpu.make_async_remote_copy(
                src_ref=bwd_mine.at[h],
                dst_ref=bwd_slots.at[h, seg],
                send_sem=bwd_send.at[h, j],
                recv_sem=bwd_recv.at[h, seg],
                device_id=(j, grp),
                device_id_type=MESH,
            ).start()
            return c

        lax.fori_loop(0, seg, give, 0)
        send_out(0, h)
        send_out(1, h)

    def part_back(h):
        carry[...] = jnp.zeros_like(carry)

        def one(j, c):
            slot = bwd_slots.at[h, j]
            pltpu.make_async_copy(slot, slot, bwd_recv.at[h, j]).wait()
            carry[...] += bwd_slots[h, j]
            return c

        lax.fori_loop(seg + 1, segs, one, 0)
        back, norm = carry[:DH, :], carry[DH : DH + 1, :]
        high, low = split(back)
        g = gate(h)
        for i in range(groups):
            here = slice(i * rows, (i + 1) * rows)
            k = gath[0, h, here, :].astype(F32)
            v = gath[1, h, here, :]
            phi = feature(k).astype(BF16)
            key = (nt(v, high) + nt(v, low) + norm) * slope(k)
            stage[2, h, here, :] = (loc[2, h, here, :] * scale + key).astype(BF16)
            value = nn(phi, high) + nn(phi, low)
            stage[3, h, here, :] = ((1.0 - g) * loc[3, h, here, :] + value).astype(BF16)
        send_out(2, h)
        send_out(3, h)

    def step(s, c):
        @pl.when(s < heads)
        def _():
            part_update(s)
            part_local(s)

        @pl.when(jnp.logical_and(s >= 1, s <= heads))
        def _():
            part_memory(s - 1)

        @pl.when(s >= 2)
        def _():
            part_back(s - 2)

        return c

    lax.fori_loop(0, heads + 2, step, 0)

    def finish(h, c):
        col = pl.multiple_of(h * DH, DH)
        for a in range(4):
            for z in range(groups):
                at = pl.multiple_of((z * heads) * DH + col, DH)
                blk = outputs[a].at[:, pl.ds(at, DH)]
                pltpu.make_async_copy(blk, blk, out_recv.at[a, h, z]).wait()
            for o in offsets:
                dest = lax.rem(grp + o, groups)
                blk = gath.at[a, h, pl.ds(0, rows), :]
                pltpu.make_async_copy(blk, blk, in_send.at[a, h, dest]).wait()
                blk = stage.at[a, h, pl.ds(0, rows), :]
                pltpu.make_async_copy(blk, blk, out_send.at[a, h, dest]).wait()

        def later(j, c):
            pltpu.make_async_copy(fwd_mine.at[h], fwd_mine.at[h], fwd_send.at[h, j]).wait()
            return c

        lax.fori_loop(seg + 1, segs, later, 0)

        def earlier(j, c):
            pltpu.make_async_copy(bwd_mine.at[h], bwd_mine.at[h], bwd_send.at[h, j]).wait()
            return c

        lax.fori_loop(0, seg, earlier, 0)
        return c

    lax.fori_loop(0, heads, finish, 0)


def body(segs, groups, queries, key_rows, values, gate_logits, out_grad):
    heads = gate_logits.shape[0]
    rows = queries.shape[0]
    length = rows * groups
    share = jnp.broadcast_to(jax.nn.sigmoid(gate_logits)[:, None, None], (heads, PAD, DH))
    any_spec = pl.BlockSpec(memory_space=pl.ANY)
    dma = pltpu.SemaphoreType.DMA
    return pl.pallas_call(
        functools.partial(kernel, segs, groups, heads),
        out_shape=[jax.ShapeDtypeStruct(queries.shape, BF16)] * 4,
        in_specs=[pl.BlockSpec(memory_space=pltpu.VMEM)] + [any_spec] * 4,
        out_specs=[any_spec] * 4,
        scratch_shapes=[
            pltpu.VMEM((4, heads, length, DH), BF16),
            pltpu.VMEM((4, heads, length, DH), BF16),
            pltpu.VMEM((4, heads, length, DH), F32),
            pltpu.VMEM((heads, DH + PAD, DH), F32),
            pltpu.VMEM((heads, segs, DH + PAD, DH), F32),
            pltpu.VMEM((heads, DH + PAD, DH), F32),
            pltpu.VMEM((heads, segs, DH + PAD, DH), F32),
            pltpu.VMEM((DH + PAD, DH), F32),
            dma((4, heads, groups)),
            dma((4, heads, groups)),
            dma((4, heads, groups)),
            dma((4, heads, groups)),
            dma((heads, segs)),
            dma((heads, segs)),
            dma((heads, segs)),
            dma((heads, segs)),
        ],
        compiler_params=pltpu.CompilerParams(collective_id=0, has_side_effects=True),
        name="infini",
    )(share, queries, key_rows, values, out_grad)


def solution(mesh):
    segs, groups = mesh.shape["seq"], mesh.shape["head"]
    tokens = P(("seq", "head"), None)
    return jax.shard_map(
        functools.partial(body, segs, groups),
        mesh=mesh,
        in_specs=(tokens, tokens, tokens, P("head"), tokens),
        out_specs=(tokens,) * 4,
        check_vma=False,
    )
```

```python
import functools

import jax
import jax.numpy as jnp
from jax import lax
from jax.experimental import pallas as pl
from jax.experimental.pallas import tpu as pltpu
from jax.sharding import PartitionSpec as P

DH = 128
PAD = 8
MESH = pl.DeviceIdType.MESH
F32 = jnp.float32
BF16 = jnp.bfloat16


def feature(x):
    return jnp.where(x > 0, x + 1.0, jnp.exp(jnp.minimum(x, 0.0)))


def slope(x):
    return jnp.where(x > 0, 1.0, jnp.exp(jnp.minimum(x, 0.0)))


def split(x):
    high = x.astype(BF16)
    return high, (x - high.astype(F32)).astype(BF16)


def nn(a, b):
    return lax.dot_general(a, b, (((1,), (0,)), ((), ())), preferred_element_type=F32)


def nt(a, b):
    return lax.dot_general(a, b, (((1,), (1,)), ((), ())), preferred_element_type=F32)


def tn(a, b):
    return lax.dot_general(a, b, (((0,), (0,)), ((), ())), preferred_element_type=F32)


def kernel(
    segs,
    groups,
    heads,
    gate_ref,
    q_in,
    k_in,
    v_in,
    d_in,
    o_out,
    q_out,
    k_out,
    v_out,
    gath,
    stage,
    loc,
    fwd_mine,
    fwd_slots,
    bwd_mine,
    bwd_slots,
    carry,
    in_send,
    in_recv,
    out_send,
    out_recv,
    fwd_send,
    fwd_recv,
    bwd_send,
    bwd_recv,
):
    seg = lax.axis_index("seq")
    grp = lax.axis_index("head")
    rows = q_in.shape[0]
    length = rows * groups
    inputs = (k_in, v_in, q_in, d_in)
    outputs = (o_out, q_out, k_out, v_out)
    scale = DH ** (-0.5)
    offsets = sorted(range(1, groups), key=lambda o: abs(2 * o - groups))

    barrier = pltpu.get_barrier_semaphore()
    for o in range(1, groups):
        pl.semaphore_signal(
            barrier, inc=1, device_id=(seg, lax.rem(grp + o, groups)), device_id_type=MESH
        )

    def greet(o, c):
        pl.semaphore_signal(
            barrier, inc=1, device_id=(lax.rem(seg + o, segs), grp), device_id_type=MESH
        )
        return c

    lax.fori_loop(1, segs, greet, 0)
    pl.semaphore_wait(barrier, groups - 1 + segs - 1)

    def in_copy(a, h, dest):
        col = pl.multiple_of((dest * heads + h) * DH, DH)
        at = pl.multiple_of(grp * rows, rows)
        return (
            inputs[a].at[:, pl.ds(col, DH)],
            gath.at[a, h, pl.ds(at, rows), :],
        )

    def send_inputs(h, c):
        for a in range(4):
            for o in offsets:
                dest = lax.rem(grp + o, groups)
                src, dst = in_copy(a, h, dest)
                pltpu.make_async_remote_copy(
                    src_ref=src,
                    dst_ref=dst,
                    send_sem=in_send.at[a, h, dest],
                    recv_sem=in_recv.at[a, h, grp],
                    device_id=(seg, dest),
                    device_id_type=MESH,
                ).start()
            src, dst = in_copy(a, h, grp)
            pltpu.make_async_copy(src, dst, in_recv.at[a, h, grp]).start()
        return c

    lax.fori_loop(0, heads, send_inputs, 0)

    def wait_inputs(a, h):
        def one(z, c):
            blk = gath.at[a, h, pl.ds(pl.multiple_of(z * rows, rows), rows), :]
            pltpu.make_async_copy(blk, blk, in_recv.at[a, h, z]).wait()
            return c

        lax.fori_loop(0, groups, one, 0)

    def send_out(a, h):
        col = pl.multiple_of((grp * heads + h) * DH, DH)
        for o in offsets:
            dest = lax.rem(grp + o, groups)
            pltpu.make_async_remote_copy(
                src_ref=stage.at[a, h, pl.ds(pl.multiple_of(dest * rows, rows), rows), :],
                dst_ref=outputs[a].at[:, pl.ds(col, DH)],
                send_sem=out_send.at[a, h, dest],
                recv_sem=out_recv.at[a, h, grp],
                device_id=(seg, dest),
                device_id_type=MESH,
            ).start()
        pltpu.make_async_copy(
            stage.at[a, h, pl.ds(pl.multiple_of(grp * rows, rows), rows), :],
            outputs[a].at[:, pl.ds(col, DH)],
            out_recv.at[a, h, grp],
        ).start()

    def gate(h):
        return 1.0 / (1.0 + jnp.exp(-jnp.full((1, DH), gate_ref[h], F32)))

    def part_update(h):
        wait_inputs(0, h)
        wait_inputs(1, h)
        phi = feature(gath[0, h].astype(F32)).astype(BF16)
        fwd_mine[h, :DH, :] = tn(phi, gath[1, h])
        fwd_mine[h, DH:, :] = jnp.broadcast_to(
            jnp.sum(phi.astype(F32), axis=0, keepdims=True), (PAD, DH)
        )

        def one(j, c):
            pltpu.make_async_remote_copy(
                src_ref=fwd_mine.at[h],
                dst_ref=fwd_slots.at[h, seg],
                send_sem=fwd_send.at[h, j],
                recv_sem=fwd_recv.at[h, seg],
                device_id=(j, grp),
                device_id_type=MESH,
            ).start()
            return c

        lax.fori_loop(seg + 1, segs, one, 0)

    def part_local(h):
        wait_inputs(2, h)
        wait_inputs(3, h)
        rest = 1.0 - gate(h)[:, :1]
        for i in range(groups - 1, -1, -1):
            first, wide = i * rows, (i + 1) * rows
            q = gath[2, h, first:wide, :]
            d = gath[3, h, first:wide, :]
            k = gath[0, h, :wide, :]
            v = gath[1, h, :wide, :]
            s = nt(q, k) * scale
            row = lax.broadcasted_iota(jnp.int32, (rows, wide), 0) + first
            col = lax.broadcasted_iota(jnp.int32, (rows, wide), 1)
            s = jnp.where(row >= col, s, -jnp.inf)
            e = jnp.exp(s - jnp.max(s, axis=-1, keepdims=True))
            w = e * (1.0 / jnp.sum(e, axis=-1, keepdims=True))
            wb = w.astype(BF16)
            dp = nt(d, v) * rest
            ds = w * (dp - jnp.sum(w * dp, axis=-1, keepdims=True))
            dsb = ds.astype(BF16)
            loc[0, h, first:wide, :] = nn(wb, v)
            loc[1, h, first:wide, :] = nn(dsb, k)
            kg = tn(dsb, q)
            vg = tn(wb, d)
            if i == groups - 1:
                loc[2, h] = kg
                loc[3, h] = vg
            else:
                loc[2, h, :wide, :] += kg
                loc[3, h, :wide, :] += vg

    def part_memory(h):
        carry[...] = jnp.zeros_like(carry)

        def one(j, c):
            slot = fwd_slots.at[h, j]
            pltpu.make_async_copy(slot, slot, fwd_recv.at[h, j]).wait()
            carry[...] += fwd_slots[h, j]
            return c

        lax.fori_loop(0, seg, one, 0)
        memory, zsum = carry[:DH, :], carry[DH : DH + 1, :]
        high, low = split(memory)
        g = gate(h)
        update = jnp.zeros((DH, DH), F32)
        norm = jnp.zeros((1, DH), F32)
        for i in range(groups):
            here = slice(i * rows, (i + 1) * rows)
            q = gath[2, h, here, :].astype(F32)
            d = gath[3, h, here, :]
            wide = d.astype(F32)
            phi = feature(q).astype(BF16)
            phi_wide = phi.astype(F32)
            raw = jnp.sum(phi_wide * zsum, axis=-1, keepdims=True)
            inv = 1.0 / jnp.maximum(raw, 1.0)
            retrieved = (nn(phi, high) + nn(phi, low)) * inv
            factor = g * inv
            numer = factor * wide
            denom = jnp.where(
                raw > 1.0,
                -g * jnp.sum(wide * retrieved, axis=-1, keepdims=True) * inv,
                0.0,
            )
            numer_high, numer_low = split(numer)
            update = update + tn(phi, numer_high) + tn(phi, numer_low)
            norm = norm + jnp.sum(denom * phi_wide, axis=0, keepdims=True)
            stage[0, h, here, :] = (g * retrieved + (1.0 - g) * loc[0, h, here, :]).astype(BF16)
            back = (nt(d, high) + nt(d, low)) * factor + denom * zsum
            stage[1, h, here, :] = (loc[1, h, here, :] * scale + back * slope(q)).astype(BF16)
        bwd_mine[h, :DH, :] = update
        bwd_mine[h, DH:, :] = jnp.broadcast_to(norm, (PAD, DH))

        def give(j, c):
            pltpu.make_async_remote_copy(
                src_ref=bwd_mine.at[h],
                dst_ref=bwd_slots.at[h, seg],
                send_sem=bwd_send.at[h, j],
                recv_sem=bwd_recv.at[h, seg],
                device_id=(j, grp),
                device_id_type=MESH,
            ).start()
            return c

        lax.fori_loop(0, seg, give, 0)
        send_out(0, h)
        send_out(1, h)

    def part_back(h):
        carry[...] = jnp.zeros_like(carry)

        def one(j, c):
            slot = bwd_slots.at[h, j]
            pltpu.make_async_copy(slot, slot, bwd_recv.at[h, j]).wait()
            carry[...] += bwd_slots[h, j]
            return c

        lax.fori_loop(seg + 1, segs, one, 0)
        back, norm = carry[:DH, :], carry[DH : DH + 1, :]
        high, low = split(back)
        g = gate(h)
        for i in range(groups):
            here = slice(i * rows, (i + 1) * rows)
            k = gath[0, h, here, :].astype(F32)
            v = gath[1, h, here, :]
            phi = feature(k).astype(BF16)
            key = (nt(v, high) + nt(v, low) + norm) * slope(k)
            stage[2, h, here, :] = (loc[2, h, here, :] * scale + key).astype(BF16)
            value = nn(phi, high) + nn(phi, low)
            stage[3, h, here, :] = ((1.0 - g) * loc[3, h, here, :] + value).astype(BF16)
        send_out(2, h)
        send_out(3, h)

    def step(s, c):
        @pl.when(s < heads)
        def _():
            part_update(s)
            part_local(s)

        @pl.when(jnp.logical_and(s >= 1, s <= heads))
        def _():
            part_memory(s - 1)

        @pl.when(s >= 2)
        def _():
            part_back(s - 2)

        return c

    lax.fori_loop(0, heads + 2, step, 0)

    def finish(h, c):
        col = pl.multiple_of(h * DH, DH)
        for a in range(4):
            for z in range(groups):
                at = pl.multiple_of((z * heads) * DH + col, DH)
                blk = outputs[a].at[:, pl.ds(at, DH)]
                pltpu.make_async_copy(blk, blk, out_recv.at[a, h, z]).wait()
            for o in offsets:
                dest = lax.rem(grp + o, groups)
                blk = gath.at[a, h, pl.ds(0, rows), :]
                pltpu.make_async_copy(blk, blk, in_send.at[a, h, dest]).wait()
                blk = stage.at[a, h, pl.ds(0, rows), :]
                pltpu.make_async_copy(blk, blk, out_send.at[a, h, dest]).wait()

        def later(j, c):
            pltpu.make_async_copy(fwd_mine.at[h], fwd_mine.at[h], fwd_send.at[h, j]).wait()
            return c

        lax.fori_loop(seg + 1, segs, later, 0)

        def earlier(j, c):
            pltpu.make_async_copy(bwd_mine.at[h], bwd_mine.at[h], bwd_send.at[h, j]).wait()
            return c

        lax.fori_loop(0, seg, earlier, 0)
        return c

    lax.fori_loop(0, heads, finish, 0)


def place(*refs):
    held, taken, put = refs[8:]
    half = refs[0].shape[0] // 2

    def pair(i):
        a, at = i // 2, pl.ds((i % 2) * half, half)
        return (
            pltpu.make_async_copy(refs[a].at[at, :], held.at[a, at, :], taken.at[i]),
            pltpu.make_async_copy(held.at[a, at, :], refs[4 + a].at[at, :], put.at[i]),
        )

    pairs = [pair(i) for i in range(8)]
    for take, _ in pairs:
        take.start()
    for take, give in pairs:
        take.wait()
        give.start()
    for _, give in pairs:
        give.wait()


def body(segs, groups, queries, key_rows, values, gate_logits, out_grad):
    heads = gate_logits.shape[0]
    rows = queries.shape[0]
    length = rows * groups
    any_spec = pl.BlockSpec(memory_space=pl.ANY)
    dma = pltpu.SemaphoreType.DMA
    results = pl.pallas_call(
        functools.partial(kernel, segs, groups, heads),
        out_shape=[jax.ShapeDtypeStruct(queries.shape, BF16)] * 4,
        in_specs=[pl.BlockSpec(memory_space=pltpu.SMEM)] + [any_spec] * 4,
        out_specs=[any_spec] * 4,
        scratch_shapes=[
            pltpu.VMEM((4, heads, length, DH), BF16),
            pltpu.VMEM((4, heads, length, DH), BF16),
            pltpu.VMEM((4, heads, length, DH), F32),
            pltpu.VMEM((heads, DH + PAD, DH), F32),
            pltpu.VMEM((heads, segs, DH + PAD, DH), F32),
            pltpu.VMEM((heads, DH + PAD, DH), F32),
            pltpu.VMEM((heads, segs, DH + PAD, DH), F32),
            pltpu.VMEM((DH + PAD, DH), F32),
            dma((4, heads, groups)),
            dma((4, heads, groups)),
            dma((4, heads, groups)),
            dma((4, heads, groups)),
            dma((heads, segs)),
            dma((heads, segs)),
            dma((heads, segs)),
            dma((heads, segs)),
        ],
        compiler_params=pltpu.CompilerParams(collective_id=0, has_side_effects=True),
        name="infini",
    )(gate_logits, queries, key_rows, values, out_grad)
    return pl.pallas_call(
        place,
        out_shape=[jax.ShapeDtypeStruct(queries.shape, BF16)] * 4,
        in_specs=[any_spec] * 4,
        out_specs=[any_spec] * 4,
        scratch_shapes=[pltpu.VMEM((4,) + queries.shape, BF16), dma((8,)), dma((8,))],
        name="place",
    )(*results)


def solution(mesh):
    segs, groups = mesh.shape["seq"], mesh.shape["head"]
    tokens = P(("seq", "head"), None)
    return jax.shard_map(
        functools.partial(body, segs, groups),
        mesh=mesh,
        in_specs=(tokens, tokens, tokens, P("head"), tokens),
        out_specs=(tokens,) * 4,
        check_vma=False,
    )
```

```python
import functools

import jax
import jax.numpy as jnp
from jax import lax
from jax.experimental import pallas as pl
from jax.experimental.pallas import tpu as pltpu
from jax.sharding import PartitionSpec as P

DH = 128
PAD = 8
MESH = pl.DeviceIdType.MESH
F32 = jnp.float32
BF16 = jnp.bfloat16


def feature(x):
    return jnp.where(x > 0, x + 1.0, jnp.exp(jnp.minimum(x, 0.0)))


def slope(x):
    return jnp.where(x > 0, 1.0, jnp.exp(jnp.minimum(x, 0.0)))


def split(x):
    high = x.astype(BF16)
    return high, (x - high.astype(F32)).astype(BF16)


def nn(a, b):
    return lax.dot_general(a, b, (((1,), (0,)), ((), ())), preferred_element_type=F32)


def nt(a, b):
    return lax.dot_general(a, b, (((1,), (1,)), ((), ())), preferred_element_type=F32)


def tn(a, b):
    return lax.dot_general(a, b, (((0,), (0,)), ((), ())), preferred_element_type=F32)


def kernel(
    segs,
    groups,
    heads,
    gate_ref,
    q_in,
    k_in,
    v_in,
    d_in,
    o_out,
    q_out,
    k_out,
    v_out,
    gath,
    stage,
    loc,
    fwd_mine,
    fwd_slots,
    bwd_mine,
    bwd_slots,
    carry,
    in_send,
    in_recv,
    out_send,
    out_recv,
    fwd_send,
    fwd_recv,
    bwd_send,
    bwd_recv,
):
    seg = lax.axis_index("seq")
    grp = lax.axis_index("head")
    rows = q_in.shape[0]
    length = rows * groups
    inputs = (k_in, v_in, q_in, d_in)
    outputs = (o_out, q_out, k_out, v_out)
    scale = DH ** (-0.5)
    offsets = sorted(range(1, groups), key=lambda o: abs(2 * o - groups))

    barrier = pltpu.get_barrier_semaphore()
    for o in range(1, groups):
        pl.semaphore_signal(
            barrier, inc=1, device_id=(seg, lax.rem(grp + o, groups)), device_id_type=MESH
        )

    def greet(o, c):
        pl.semaphore_signal(
            barrier, inc=1, device_id=(lax.rem(seg + o, segs), grp), device_id_type=MESH
        )
        return c

    lax.fori_loop(1, segs, greet, 0)
    pl.semaphore_wait(barrier, groups - 1 + segs - 1)

    def in_copy(a, h, dest):
        col = pl.multiple_of((dest * heads + h) * DH, DH)
        at = pl.multiple_of(grp * rows, rows)
        return (
            inputs[a].at[:, pl.ds(col, DH)],
            gath.at[a, h, pl.ds(at, rows), :],
        )

    def send_inputs(h, c):
        for a in range(4):
            for o in offsets:
                dest = lax.rem(grp + o, groups)
                src, dst = in_copy(a, h, dest)
                pltpu.make_async_remote_copy(
                    src_ref=src,
                    dst_ref=dst,
                    send_sem=in_send.at[a, h, dest],
                    recv_sem=in_recv.at[a, h, grp],
                    device_id=(seg, dest),
                    device_id_type=MESH,
                ).start()
            src, dst = in_copy(a, h, grp)
            pltpu.make_async_copy(src, dst, in_recv.at[a, h, grp]).start()
        return c

    lax.fori_loop(0, heads, send_inputs, 0)

    def wait_inputs(a, h):
        def one(z, c):
            blk = gath.at[a, h, pl.ds(pl.multiple_of(z * rows, rows), rows), :]
            pltpu.make_async_copy(blk, blk, in_recv.at[a, h, z]).wait()
            return c

        lax.fori_loop(0, groups, one, 0)

    def send_out(a, h):
        col = pl.multiple_of((grp * heads + h) * DH, DH)
        for o in offsets:
            dest = lax.rem(grp + o, groups)
            pltpu.make_async_remote_copy(
                src_ref=stage.at[a, h, pl.ds(pl.multiple_of(dest * rows, rows), rows), :],
                dst_ref=outputs[a].at[:, pl.ds(col, DH)],
                send_sem=out_send.at[a, h, dest],
                recv_sem=out_recv.at[a, h, grp],
                device_id=(seg, dest),
                device_id_type=MESH,
            ).start()
        pltpu.make_async_copy(
            stage.at[a, h, pl.ds(pl.multiple_of(grp * rows, rows), rows), :],
            outputs[a].at[:, pl.ds(col, DH)],
            out_recv.at[a, h, grp],
        ).start()

    def gate(h):
        return 1.0 / (1.0 + jnp.exp(-jnp.full((1, DH), gate_ref[h], F32)))

    def part_update(h):
        wait_inputs(0, h)
        wait_inputs(1, h)
        phi = feature(gath[0, h].astype(F32)).astype(BF16)
        fwd_mine[h, :DH, :] = tn(phi, gath[1, h])
        fwd_mine[h, DH:, :] = jnp.broadcast_to(
            jnp.sum(phi.astype(F32), axis=0, keepdims=True), (PAD, DH)
        )

        def one(j, c):
            pltpu.make_async_remote_copy(
                src_ref=fwd_mine.at[h],
                dst_ref=fwd_slots.at[h, seg],
                send_sem=fwd_send.at[h, j],
                recv_sem=fwd_recv.at[h, seg],
                device_id=(j, grp),
                device_id_type=MESH,
            ).start()
            return c

        lax.fori_loop(seg + 1, segs, one, 0)

    def part_local(h):
        wait_inputs(2, h)
        wait_inputs(3, h)
        rest = 1.0 - gate(h)[:, :1]
        for i in range(groups - 1, -1, -1):
            first, wide = i * rows, (i + 1) * rows
            q = gath[2, h, first:wide, :]
            d = gath[3, h, first:wide, :]
            k = gath[0, h, :wide, :]
            v = gath[1, h, :wide, :]
            s = nt(q, k) * scale
            row = lax.broadcasted_iota(jnp.int32, (rows, wide), 0) + first
            col = lax.broadcasted_iota(jnp.int32, (rows, wide), 1)
            s = jnp.where(row >= col, s, -jnp.inf)
            e = jnp.exp(s - jnp.max(s, axis=-1, keepdims=True))
            w = e * (1.0 / jnp.sum(e, axis=-1, keepdims=True))
            wb = w.astype(BF16)
            dp = nt(d, v) * rest
            ds = w * (dp - jnp.sum(w * dp, axis=-1, keepdims=True))
            dsb = ds.astype(BF16)
            loc[0, h, first:wide, :] = nn(wb, v)
            loc[1, h, first:wide, :] = nn(dsb, k)
            kg = tn(dsb, q)
            vg = tn(wb, d)
            if i == groups - 1:
                loc[2, h] = kg
                loc[3, h] = vg
            else:
                loc[2, h, :wide, :] += kg
                loc[3, h, :wide, :] += vg

    def part_memory(h):
        carry[...] = jnp.zeros_like(carry)

        def one(j, c):
            slot = fwd_slots.at[h, j]
            pltpu.make_async_copy(slot, slot, fwd_recv.at[h, j]).wait()
            carry[...] += fwd_slots[h, j]
            return c

        lax.fori_loop(0, seg, one, 0)
        memory, zsum = carry[:DH, :], carry[DH : DH + 1, :]
        high, low = split(memory)
        g = gate(h)
        update = jnp.zeros((DH, DH), F32)
        norm = jnp.zeros((1, DH), F32)
        for i in range(groups):
            here = slice(i * rows, (i + 1) * rows)
            q = gath[2, h, here, :].astype(F32)
            d = gath[3, h, here, :]
            wide = d.astype(F32)
            phi = feature(q).astype(BF16)
            phi_wide = phi.astype(F32)
            raw = jnp.sum(phi_wide * zsum, axis=-1, keepdims=True)
            inv = 1.0 / jnp.maximum(raw, 1.0)
            retrieved = (nn(phi, high) + nn(phi, low)) * inv
            factor = g * inv
            numer = factor * wide
            denom = jnp.where(
                raw > 1.0,
                -g * jnp.sum(wide * retrieved, axis=-1, keepdims=True) * inv,
                0.0,
            )
            numer_high, numer_low = split(numer)
            update = update + tn(phi, numer_high) + tn(phi, numer_low)
            norm = norm + jnp.sum(denom * phi_wide, axis=0, keepdims=True)
            stage[0, h, here, :] = (g * retrieved + (1.0 - g) * loc[0, h, here, :]).astype(BF16)
            back = (nt(d, high) + nt(d, low)) * factor + denom * zsum
            stage[1, h, here, :] = (loc[1, h, here, :] * scale + back * slope(q)).astype(BF16)
        bwd_mine[h, :DH, :] = update
        bwd_mine[h, DH:, :] = jnp.broadcast_to(norm, (PAD, DH))

        def give(j, c):
            pltpu.make_async_remote_copy(
                src_ref=bwd_mine.at[h],
                dst_ref=bwd_slots.at[h, seg],
                send_sem=bwd_send.at[h, j],
                recv_sem=bwd_recv.at[h, seg],
                device_id=(j, grp),
                device_id_type=MESH,
            ).start()
            return c

        lax.fori_loop(0, seg, give, 0)
        send_out(0, h)
        send_out(1, h)

    def part_back(h):
        carry[...] = jnp.zeros_like(carry)

        def one(j, c):
            slot = bwd_slots.at[h, j]
            pltpu.make_async_copy(slot, slot, bwd_recv.at[h, j]).wait()
            carry[...] += bwd_slots[h, j]
            return c

        lax.fori_loop(seg + 1, segs, one, 0)
        back, norm = carry[:DH, :], carry[DH : DH + 1, :]
        high, low = split(back)
        g = gate(h)
        for i in range(groups):
            here = slice(i * rows, (i + 1) * rows)
            k = gath[0, h, here, :].astype(F32)
            v = gath[1, h, here, :]
            phi = feature(k).astype(BF16)
            key = (nt(v, high) + nt(v, low) + norm) * slope(k)
            stage[2, h, here, :] = (loc[2, h, here, :] * scale + key).astype(BF16)
            value = nn(phi, high) + nn(phi, low)
            stage[3, h, here, :] = ((1.0 - g) * loc[3, h, here, :] + value).astype(BF16)
        send_out(2, h)
        send_out(3, h)

    def step(s, c):
        @pl.when(s < heads)
        def _():
            part_update(s)
            part_local(s)

        @pl.when(jnp.logical_and(s >= 1, s <= heads))
        def _():
            part_memory(s - 1)

        @pl.when(s >= 2)
        def _():
            part_back(s - 2)

        return c

    lax.fori_loop(0, heads + 2, step, 0)

    def finish(h, c):
        col = pl.multiple_of(h * DH, DH)
        for a in range(4):
            for z in range(groups):
                at = pl.multiple_of((z * heads) * DH + col, DH)
                blk = outputs[a].at[:, pl.ds(at, DH)]
                pltpu.make_async_copy(blk, blk, out_recv.at[a, h, z]).wait()
            for o in offsets:
                dest = lax.rem(grp + o, groups)
                blk = gath.at[a, h, pl.ds(0, rows), :]
                pltpu.make_async_copy(blk, blk, in_send.at[a, h, dest]).wait()
                blk = stage.at[a, h, pl.ds(0, rows), :]
                pltpu.make_async_copy(blk, blk, out_send.at[a, h, dest]).wait()

        def later(j, c):
            pltpu.make_async_copy(fwd_mine.at[h], fwd_mine.at[h], fwd_send.at[h, j]).wait()
            return c

        lax.fori_loop(seg + 1, segs, later, 0)

        def earlier(j, c):
            pltpu.make_async_copy(bwd_mine.at[h], bwd_mine.at[h], bwd_send.at[h, j]).wait()
            return c

        lax.fori_loop(0, seg, earlier, 0)
        return c

    lax.fori_loop(0, heads, finish, 0)


def place(*refs):
    done = refs[8]
    copies = [pltpu.make_async_copy(refs[i], refs[4 + i], done.at[i]) for i in range(4)]
    for copy in copies:
        copy.start()
    for copy in copies:
        copy.wait()


def body(segs, groups, queries, key_rows, values, gate_logits, out_grad):
    heads = gate_logits.shape[0]
    rows = queries.shape[0]
    length = rows * groups
    any_spec = pl.BlockSpec(memory_space=pl.ANY)
    dma = pltpu.SemaphoreType.DMA
    results = pl.pallas_call(
        functools.partial(kernel, segs, groups, heads),
        out_shape=[jax.ShapeDtypeStruct(queries.shape, BF16)] * 4,
        in_specs=[pl.BlockSpec(memory_space=pltpu.SMEM)] + [any_spec] * 4,
        out_specs=[any_spec] * 4,
        scratch_shapes=[
            pltpu.VMEM((4, heads, length, DH), BF16),
            pltpu.VMEM((4, heads, length, DH), BF16),
            pltpu.VMEM((4, heads, length, DH), F32),
            pltpu.VMEM((heads, DH + PAD, DH), F32),
            pltpu.VMEM((heads, segs, DH + PAD, DH), F32),
            pltpu.VMEM((heads, DH + PAD, DH), F32),
            pltpu.VMEM((heads, segs, DH + PAD, DH), F32),
            pltpu.VMEM((DH + PAD, DH), F32),
            dma((4, heads, groups)),
            dma((4, heads, groups)),
            dma((4, heads, groups)),
            dma((4, heads, groups)),
            dma((heads, segs)),
            dma((heads, segs)),
            dma((heads, segs)),
            dma((heads, segs)),
        ],
        compiler_params=pltpu.CompilerParams(collective_id=0, has_side_effects=True, vmem_limit_bytes=49 * 1024 * 1024),
        name="infini",
    )(gate_logits, queries, key_rows, values, out_grad)
    return pl.pallas_call(
        place,
        out_shape=[jax.ShapeDtypeStruct(queries.shape, BF16)] * 4,
        in_specs=[any_spec] * 4,
        out_specs=[pl.BlockSpec(memory_space=pltpu.HBM)] * 4,
        scratch_shapes=[dma((4,))],
        compiler_params=pltpu.CompilerParams(vmem_limit_bytes=4 * 1024 * 1024),
        name="place",
    )(*results)


def solution(mesh):
    segs, groups = mesh.shape["seq"], mesh.shape["head"]
    tokens = P(("seq", "head"), None)
    return jax.shard_map(
        functools.partial(body, segs, groups),
        mesh=mesh,
        in_specs=(tokens, tokens, tokens, P("head"), tokens),
        out_specs=(tokens,) * 4,
        check_vma=False,
    )
```
